32 devices in a mesh: rep: 2 (over core), space: 16 (over z, y, x).
Axes of the slice: x: 2, y: 2, z: 4, core: 2. Of those that a mesh axis runs over, the one named last changes fastest.
Arguments:
- particles: float32 [6, 2, 8192, 128], P(None, 'rep', 'space'), may hold values from -6 to 6
- pair_order: int32 [2, 8192, 128], P('rep', 'space'), may hold values from 0 to 127, each once within a row
- accepted: int32 [2, 8192, 64], P('rep', 'space'), may hold values 0 or 1
- direction: int32 [2, 8192, 64], P('rep', 'space'), may hold values from 0 to 255
- destination: int32 [2, 8192], P('rep', 'space'), may hold values from 0 to 15, as said below
- live_count: int32 [2, 16], P('rep', 'space'), may hold values from 256 to 512, as said below
- cell_index: int32 [2, 8192], P('rep', 'space'), may hold values from 0 to 255
Outputs:
- moved: float32 [6, 2, 12288, 128], P(None, 'rep', 'space')
- samples: float32 [4, 16, 256], P(None, 'space', 'rep')
The draws below stay inside these ranges and needn't reach their ends.
Inputs may be any that keep to these rules, and one draw needn't show every extreme that they name: Every block's destination is its own slab or one of the two beside it, slab 0 and slab 16 - 1 being beside each other; only live blocks leave; one slab of one replica sends at most 128 blocks to each of its two neighbours, and in every replica some slab sends exactly 128 to its upper and some slab exactly 128 to its lower neighbour. `live_count`: the count of live blocks of each slab of each replica; slab 0 of replica 0 is full.
All inputs are finite; a program needn't handle non-finite values. No bound on the sum of `accepted` on one device may be relied on, other than what follows from the above.
Results may differ from the reference program's by a relative error of at most 0.0003.
Values sent between devices are 32-bit elements; how exact they have to be, the bound alone decides.
A program may use at most 64 MiB of HBM per device.

```python
import jax
import jax.numpy as jnp
from jax import lax

PART = 128
PAIRS = 64
NDIR = 256
CAP = 512
MOVE = 128
CELLS = 256
OUTCAP = 768
REPS = 2
SLABS = 16
BLOCKS = 8192


def migration_plan(key):
    count_key = jax.random.fold_in(key, 101)
    upper_key = jax.random.fold_in(key, 102)
    upper_full = jax.random.fold_in(key, 103)
    lower_key = jax.random.fold_in(key, 104)
    lower_full = jax.random.fold_in(key, 105)
    order_key = jax.random.fold_in(key, 106)
    slab_ids = jnp.arange(SLABS, dtype=jnp.int32)[None, :]
    replica_ids = jnp.arange(REPS, dtype=jnp.int32)[:, None]
    living = jax.random.randint(count_key, (REPS, SLABS), CAP // 2, CAP + 1)
    living = jnp.where((slab_ids == 0) & (replica_ids == 0), CAP, living)
    upward = jax.random.randint(upper_key, (REPS, SLABS), 0, MOVE + 1)
    upward = jnp.where(slab_ids == jax.random.randint(upper_full, (REPS, 1), 0, SLABS), MOVE, upward)
    downward = jax.random.randint(lower_key, (REPS, SLABS), 0, MOVE + 1)
    downward = jnp.where(slab_ids == jax.random.randint(lower_full, (REPS, 1), 0, SLABS), MOVE, downward)
    slots = jnp.arange(CAP, dtype=jnp.int32)[None, None, :]
    noise = jax.random.randint(order_key, (REPS, SLABS, CAP), 0, 2 ** 18)
    priority = noise * CAP + slots + jnp.where(slots < living[:, :, None], 0, 2 ** 30)
    ranking = jnp.argsort(jnp.argsort(priority, axis=-1), axis=-1)
    offset = jnp.where(ranking < upward[:, :, None], 1, jnp.where(ranking < (upward + downward)[:, :, None], SLABS - 1, 0))
    target = (slab_ids[:, :, None] + offset) % SLABS
    return (living.astype(jnp.int32), target.reshape(REPS, SLABS * CAP).astype(jnp.int32))


def draw_destination(key, part):
    return migration_plan(key)[1]


def draw_live_count(key, part):
    return migration_plan(key)[0]


def place_ends(values, own_key, smallest, largest):
    index_at = [jax.random.randint(jax.random.fold_in(own_key, axis), (), 0, length) for axis, length in enumerate(values.shape)]
    widest = values.shape.index(max(values.shape))
    beside = index_at[:widest] + [(index_at[widest] + 1) % values.shape[widest]] + index_at[widest + 1:]
    return values.at[tuple(index_at)].set(smallest).at[tuple(beside)].set(largest)


def block_scale(stream_key, shape, split, least, largest):
    def one(axis_at, shards_of):
        steps = jax.random.uniform(jax.random.fold_in(jax.random.fold_in(stream_key, 6), axis_at), (shards_of,), jnp.float32, least / len(split), largest / len(split))
        return jnp.repeat(jnp.exp(steps), shape[axis_at] // shards_of).reshape((-1,) + (1,) * (len(shape) - axis_at - 1))

    level = one(*split[0])
    for cut in split[1:]:
        level = level * one(*cut)
    return level


def bell_draw(key, shape, spread, most, pieces=(), held_as=jnp.bfloat16):
    factor_of = block_scale(key, shape, pieces, -0.22, 0.18) if pieces else 1.0
    array = jax.random.normal(key, shape, jnp.float32) * spread * factor_of
    return jnp.minimum(jnp.maximum(array, -most), most).astype(held_as)


def setup_inputs(seed: int = 0) -> dict:
    keys = jax.random.split(jax.random.key(seed), 8)
    return {
        "particles": bell_draw(keys[0], (6, REPS, BLOCKS, PART), 1.0, 6.0, ((1, 2), (2, 16)), jnp.float32),
        "pair_order": jax.vmap(lambda own: jax.random.permutation(own, PART))(jax.random.split(keys[1], REPS * BLOCKS)).reshape((REPS, BLOCKS, PART)).astype(jnp.int32),
        "accepted": place_ends((jax.random.randint(keys[2], (REPS, BLOCKS, PAIRS), 0, 2) < 1).astype(jnp.int32), jax.random.fold_in(keys[2], 1), 0, 1),
        "direction": place_ends(jax.random.randint(keys[3], (REPS, BLOCKS, PAIRS), 0, NDIR), jax.random.fold_in(keys[3], 1), 0, NDIR - 1).astype(jnp.int32),
        "destination": draw_destination(jax.random.fold_in(keys[7], 71), 0),
        "live_count": draw_live_count(jax.random.fold_in(keys[7], 71), 0),
        "cell_index": place_ends(jax.random.randint(keys[6], (REPS, BLOCKS), 0, CELLS), jax.random.fold_in(keys[6], 1), 0, CELLS - 1).astype(jnp.int32),
    }


time_step = 0.25
golden_turn = 2.399963229728653

def directions(index):
    turns = index.astype(jnp.float32)
    height = 1.0 - (2.0 * turns + 1.0) / NDIR
    radius = jnp.sqrt(1.0 - height * height)
    angle = turns * golden_turn
    return jnp.stack([radius * jnp.cos(angle), radius * jnp.sin(angle), height])

def place_block(values, order):
    return jnp.zeros_like(values).at[:, order].set(values)

def collide(velocity, pair_order, accepted, direction):
    permuted = jnp.take_along_axis(velocity, pair_order[None], axis=2)
    first = permuted[:, :, :PAIRS]
    second = permuted[:, :, PAIRS:]
    center = 0.5 * (first + second)
    relative = first - second
    speed = jnp.sqrt(lax.optimization_barrier(jnp.sum(relative * relative, axis=0)))
    unit = directions(direction)
    taken = (accepted == 1)[None]
    first_out = jnp.where(taken, center + 0.5 * speed * unit, first)
    second_out = jnp.where(taken, center - 0.5 * speed * unit, second)
    combined = jnp.concatenate([first_out, second_out], axis=2)
    return jax.vmap(place_block, in_axes=(1, 0), out_axes=1)(combined, pair_order)

def moments(velocity, living):
    sums = jnp.stack([lax.optimization_barrier(jnp.sum(velocity[0], axis=1)), lax.optimization_barrier(jnp.sum(velocity[1], axis=1)), lax.optimization_barrier(jnp.sum(velocity[2], axis=1)), lax.optimization_barrier(jnp.sum(lax.optimization_barrier(jnp.sum(velocity * velocity, axis=0)), axis=1))])
    return jnp.where(living[None], sums, 0.0)

def select_movers(updated, moving):
    ranking = jnp.cumsum(moving.astype(jnp.int32)) - 1
    slots = jnp.arange(MOVE, dtype=jnp.int32)
    matches = moving[None, :] & (ranking[None, :] == slots[:, None])
    sources = jnp.arange(moving.shape[0], dtype=jnp.int32)
    chosen = lax.optimization_barrier(jnp.sum(jnp.where(matches, sources[None, :], 0), axis=1)).astype(jnp.int32)
    is_valid = jnp.any(matches, axis=1)
    return jnp.where(is_valid[None, :, None], jnp.take(updated, chosen, axis=1), 0.0)

def one_replica(inputs):
    particles, pair_order, accepted, direction, destination, live_count, cell_index = inputs
    velocity = collide(particles[3:], pair_order, accepted, direction)
    position = particles[:3] + time_step * velocity
    updated = jnp.concatenate([position, velocity], axis=0)
    block_ids = jnp.arange(BLOCKS, dtype=jnp.int32)
    slot_index = block_ids % CAP
    slab_index = block_ids // CAP
    living = slot_index < live_count[slab_index]
    to_upper = living & (destination == (slab_index + 1) % SLABS)
    to_lower = living & (destination == (slab_index + SLABS - 1) % SLABS)
    staying = living & (destination == slab_index)
    term = moments(velocity, living)
    sampled = jax.ops.segment_sum(term.T, slab_index * CELLS + cell_index, num_segments=SLABS * CELLS)
    by_slab = updated.reshape(6, SLABS, CAP, PART)
    send_upper = jax.vmap(select_movers, in_axes=(1, 0), out_axes=1)(by_slab, to_upper.reshape(SLABS, CAP))
    send_lower = jax.vmap(select_movers, in_axes=(1, 0), out_axes=1)(by_slab, to_lower.reshape(SLABS, CAP))
    from_lower = jnp.roll(send_upper, 1, axis=1)
    from_upper = jnp.roll(send_lower, -1, axis=1)
    own_blocks = jnp.where(staying.reshape(SLABS, CAP)[None, :, :, None], by_slab, 0.0)
    moved = jnp.concatenate([from_lower, own_blocks, from_upper], axis=2).reshape(6, SLABS * OUTCAP, PART)
    return (moved, sampled.T)

def reference(particles, pair_order, accepted, direction, destination, live_count, cell_index):
    inputs = (jnp.moveaxis(particles, 1, 0), pair_order, accepted, direction, destination, live_count, cell_index)
    moved, sampled = lax.map(one_replica, inputs)
    moved = jnp.moveaxis(moved, 0, 1)
    samples = (lax.optimization_barrier(jnp.sum(sampled, axis=0)) / (PART * REPS)).reshape(4, SLABS, CELLS)
    return (moved, samples)
```

```python
import functools

import jax
import jax.numpy as jnp
from jax import lax
from jax.experimental import pallas as pl
from jax.experimental.pallas import tpu as pltpu
from jax.sharding import PartitionSpec as P

NDIR = 256
MOVE = 128
CELLS = 256
TIME_STEP = 0.25
GOLDEN_TURN = 2.399963229728653


def take_lanes(values, index):
    return jnp.take_along_axis(values, index, axis=1, mode="promise_in_bounds")


def split3(value):
    high = value.astype(jnp.bfloat16)
    rest = value - high.astype(jnp.float32)
    middle = rest.astype(jnp.bfloat16)
    low = (rest - middle.astype(jnp.float32)).astype(jnp.bfloat16)
    return high, middle, low


def split2(value):
    high = value.astype(jnp.bfloat16)
    return high, (value - high.astype(jnp.float32)).astype(jnp.bfloat16)


def dot(left, right):
    return jnp.dot(left, right, preferred_element_type=jnp.float32)


def dot_nt(left, right):
    return lax.dot_general(left, right, (((1,), (1,)), ((), ())), preferred_element_type=jnp.float32)


def inverse_order(order):
    chunk, part = order.shape
    count = part // 8
    lane = lax.broadcasted_iota(jnp.int32, (chunk, part), 1)
    keys = jnp.transpose((order * part + lane).astype(jnp.float32))
    rows = [keys[8 * i:8 * i + 8] for i in range(count)]
    sublane = lax.broadcasted_iota(jnp.int32, (8, chunk), 0)
    sign = None
    size = 2
    while size <= part:
        wanted = None
        if count <= size < part:
            wanted = jnp.where((sublane & (size // count)) == 0, 1.0, -1.0)
        if sign is not None or wanted is not None:
            flip = wanted if sign is None else sign if wanted is None else sign * wanted
            rows = [row * flip for row in rows]
        sign = wanted
        stride = size // 2
        while stride >= 1:
            if stride >= count:
                apart = stride // count
                is_low = (sublane & apart) == 0
                swapped = [jnp.take_along_axis(row, sublane ^ apart, axis=0, mode="promise_in_bounds") for row in rows]
                rows = [jnp.where(is_low, jnp.minimum(r, o), jnp.maximum(r, o)) for r, o in zip(rows, swapped)]
            else:
                after = list(rows)
                for i in range(count):
                    j = i ^ stride
                    rising = size >= count or (i & size) == 0
                    pick = jnp.minimum if (i < j) == rising else jnp.maximum
                    after[i] = pick(rows[i], rows[j])
                rows = after
            stride //= 2
        size *= 2
    ranked = [(row - ((sublane * count + i) * part).astype(jnp.float32)) for i, row in enumerate(rows)]
    placed = jnp.transpose(jnp.concatenate(ranked, axis=0)).astype(jnp.int32)
    return take_lanes(placed, (lane & (count - 1)) * 8 + lane // count)


def pick_rows(chosen, pieces):
    part = pieces[0].shape[1]
    both = dot(chosen, jnp.concatenate(pieces, axis=1))
    return both[:, :part] + both[:, part:]


def choose_movers(dest_ref, live, goals, chosen_ref):
    cap = dest_ref.shape[1]
    chunk = MOVE
    count = cap // chunk
    lane = lax.broadcasted_iota(jnp.int32, (1, chunk), 1)
    flags = []
    for goal in goals:
        for i in range(count):
            here = dest_ref[:, i * chunk:(i + 1) * chunk]
            flags.append(jnp.where((here == goal) & (lane + i * chunk < live), 1.0, 0.0))
    flags = jnp.concatenate(flags, axis=0)
    row = lax.broadcasted_iota(jnp.int32, (chunk, 2 * chunk), 0)
    column = lax.broadcasted_iota(jnp.int32, (chunk, 2 * chunk), 1)
    sums = jnp.where((row <= column), 1.0, 0.0).astype(jnp.bfloat16)
    counted = dot(flags.astype(jnp.bfloat16), sums)
    slot = lax.broadcasted_iota(jnp.int32, (chunk, chunk), 0)
    for j in range(2):
        before = jnp.zeros((1, chunk), jnp.float32)
        for i in range(count):
            at = j * count + i
            rank = counted[at:at + 1, :chunk] + before
            place = jnp.where(flags[at:at + 1] > 0.0, rank - 1.0, -1.0).astype(jnp.int32)
            chosen_ref[pl.ds(j * MOVE, MOVE), pl.ds(i * chunk, chunk)] = jnp.where(slot == place, 1.0, 0.0).astype(jnp.bfloat16)
            before = before + counted[at:at + 1, chunk:]


def main_kernel(slabs, part_hbm, order_hbm, flag_hbm, turn_hbm, dest_hbm, live_ref, cell_hbm,
                moved_ref, samples_ref, part_ref, order_ref, flag_ref, turn_ref, dest_ref, cell_ref,
                table, packed_t, keep_t, inverse_t, parts, square, chosen_ref,
                sent_place, sent_speed, got_place, got_speed, sent_cells, got_cells,
                load_sem, send_sem, recv_sem, far_sem):
    cap, part = order_ref.shape
    chunk = MOVE
    steps = cap // chunk
    pairs = part // 2
    reps, _, share = sent_cells.shape
    my_slab = lax.axis_index("space")
    my_rep = lax.axis_index("rep")
    odd = lax.rem(my_slab, 2)
    near = odd
    far = 1 - odd
    near_slab = my_slab + 1 - 2 * odd
    far_slab = lax.rem(my_slab + slabs - 1 + 2 * odd, slabs)
    goals = (lax.rem(my_slab + 1, slabs), lax.rem(my_slab + slabs - 1, slabs))
    is_end = (my_slab == 0) | (my_slab == slabs - 1)
    middle = slabs // 2 - 1
    is_middle = my_slab == middle
    is_first = my_slab == 1
    live = live_ref[0, 0]

    loads = []

    def load(source, target):
        each = pltpu.make_async_copy(source, target, load_sem.at[len(loads)])
        each.start()
        loads.append(each)
        return each

    dest_load = load(dest_hbm, dest_ref)
    place_loads = [load(part_hbm.at[k], part_ref.at[k]) for k in range(3)]
    turn_load = load(turn_hbm, turn_ref)
    flag_load = load(flag_hbm, flag_ref)
    order_load = load(order_hbm, order_ref)
    speed_load = load(part_hbm.at[pl.ds(3, 3)], part_ref.at[pl.ds(3, 3)])
    cell_load = load(cell_hbm, cell_ref)

    def copy(source, target, k, device):
        return pltpu.make_async_remote_copy(
            src_ref=source, dst_ref=target, send_sem=send_sem.at[k], recv_sem=recv_sem.at[k],
            device_id=device, device_id_type=pl.DeviceIdType.MESH,
        )

    def mover_copies(sent, got, base, j, device):
        return [copy(sent.at[j, k], got.at[j, k], base + 3 * j + k, {"space": device}) for k in range(3)]

    place_far = mover_copies(sent_place, got_place, 0, far, far_slab)
    place_near = mover_copies(sent_place, got_place, 0, near, near_slab)
    speed_far = mover_copies(sent_speed, got_speed, 6, far, far_slab)
    speed_near = mover_copies(sent_speed, got_speed, 6, near, near_slab)
    cell_copies = [
        copy(sent_cells.at[k], got_cells.at[k], 11 + k, {"rep": lax.rem(my_rep + k, reps)}) for k in range(1, reps)
    ]

    def start(copies):
        for each in copies:
            each.start()

    barrier = pltpu.get_barrier_semaphore()

    def greet(**device):
        pl.semaphore_signal(barrier, inc=1, device_id=device, device_id_type=pl.DeviceIdType.MESH)

    greet(space=near_slab)
    for k in range(1, reps):
        greet(rep=lax.rem(my_rep + k, reps))

    @pl.when(is_end)
    def _():
        greet(space=middle)

    @pl.when(jnp.logical_not(is_end))
    def _():
        greet(space=far_slab)

    dest_load.wait()
    choose_movers(dest_ref, live, goals, chosen_ref)
    for k in range(3):
        place_loads[k].wait()
        sent = pick_rows(chosen_ref[...], split2(part_ref[k]))
        sent_place[0, k] = sent[:MOVE]
        sent_place[1, k] = sent[MOVE:]
        if k == 0:
            @pl.when(is_end)
            def _():
                pl.semaphore_wait(barrier, reps)

            @pl.when(is_middle)
            def _():
                pl.semaphore_wait(barrier, 3 + reps)
                for end in (0, slabs - 1):
                    pl.semaphore_signal(far_sem, inc=1, device_id={"space": end}, device_id_type=pl.DeviceIdType.MESH)

            @pl.when(jnp.logical_not(is_end | is_middle))
            def _():
                pl.semaphore_wait(barrier, 1 + reps)

        @pl.when(jnp.logical_not(is_end | is_first))
        def _(k=k):
            place_far[k].start()

        place_near[k].start()

        @pl.when(is_first)
        def _(k=k):
            place_far[k].start()

    for half in range(2):
        turns = (lax.broadcasted_iota(jnp.int32, (8, part), 1) + half * part).astype(jnp.float32)
        height = 1.0 - (2.0 * turns + 1.0) / NDIR
        radius = jnp.sqrt(1.0 - height * height)
        angle = turns * GOLDEN_TURN
        table[half] = radius * jnp.cos(angle)
        table[half + 2] = radius * jnp.sin(angle)

    turn_load.wait()
    flag_load.wait()
    order_load.wait()
    speed_load.wait()

    def chunk_step(step, carry):
        at = pl.multiple_of(step * chunk, chunk)
        here = pl.ds(at, chunk)
        pair_code = turn_ref[:, here] + NDIR * flag_ref[:, here]
        packed_t[...] = jnp.transpose(jnp.concatenate([pair_code, pair_code], axis=0))
        slots = lax.broadcasted_iota(jnp.int32, (1, chunk), 1) + at
        staying = (dest_ref[:, here] == my_slab) & (slots < live)
        stay_rows = jnp.broadcast_to(jnp.where(staying, 1.0, 0.0), (part, chunk))
        keep_t[...] = jnp.transpose(stay_rows)
        inverse_t[...] = inverse_order(order_ref[here, :])

        order = order_ref[here, :]
        inverse = inverse_t[...]
        partner = take_lanes(order, inverse ^ pairs)
        code = take_lanes(packed_t[...], inverse & (pairs - 1))
        taken = code >= NDIR
        turn = code & (NDIR - 1)
        low_index = turn & (part - 1)
        is_high = turn >= part
        wide = (chunk, part)
        tables = [jnp.broadcast_to(table[k, 0:1, :], wide) for k in range(4)]
        unit_x = jnp.where(is_high, take_lanes(tables[1], low_index), take_lanes(tables[0], low_index))
        unit_y = jnp.where(is_high, take_lanes(tables[3], low_index), take_lanes(tables[2], low_index))
        unit_z = 1.0 - (2.0 * turn.astype(jnp.float32) + 1.0) / NDIR
        old = [part_ref[3 + k, here, :] for k in range(3)]
        other = [take_lanes(v, partner) for v in old]
        relative = [a - b for a, b in zip(old, other)]
        speed = jnp.sqrt(relative[0] * relative[0] + relative[1] * relative[1] + relative[2] * relative[2])
        half_speed = jnp.where(inverse < pairs, 0.5, -0.5) * speed
        new = [
            jnp.where(taken, 0.5 * (a + b) + half_speed * u, a)
            for a, b, u in zip(old, other, (unit_x, unit_y, unit_z))
        ]
        keep = keep_t[...] > 0.0
        target = pl.ds(pl.multiple_of(MOVE + at, chunk), chunk)
        square[here, :] = new[0] * new[0] + new[1] * new[1] + new[2] * new[2]
        for k in range(3):
            moved_ref[k, target, :] = jnp.where(keep, part_ref[k, here, :] + TIME_STEP * new[k], 0.0)
            moved_ref[3 + k, target, :] = jnp.where(keep, new[k], 0.0)
            for j, piece in enumerate(split3(new[k])):
                parts[j, here, pl.ds(k * part, part)] = piece

        @pl.when((step == 0) & is_end)
        def _():
            pl.semaphore_wait(far_sem, 1)
            start(place_far)

        return carry

    lax.fori_loop(0, steps, chunk_step, 0)

    for k in range(3):
        sent = pick_rows(chosen_ref[...], [parts[j, :, pl.ds(k * part, part)] for j in range(2)])
        sent_speed[0, k] = sent[:MOVE]
        sent_speed[1, k] = sent[MOVE:]

        @pl.when(jnp.logical_not(is_first))
        def _(k=k):
            speed_far[k].start()

        @pl.when(jnp.logical_not(is_end))
        def _(k=k):
            speed_near[k].start()

    @pl.when(is_end)
    def _():
        start(speed_near)

    @pl.when(is_first)
    def _():
        start(speed_far)

    cell_load.wait()
    living = lax.broadcasted_iota(jnp.int32, (1, cap), 1) < live
    ones = jnp.ones((8, part), jnp.bfloat16)
    eight = lax.broadcasted_iota(jnp.int32, (8, cap), 0)
    terms = []
    for k in range(3):
        here = pl.ds(k * part, part)
        terms.append(dot_nt(ones, parts[0, :, here]) + dot_nt(ones, parts[1, :, here]) + dot_nt(ones, parts[2, :, here]))
    pieces = split3(square[...])
    terms.append(dot_nt(ones, pieces[0]) + dot_nt(ones, pieces[1]) + dot_nt(ones, pieces[2]))
    term = jnp.where(eight == 0, terms[0], jnp.where(eight == 1, terms[1], jnp.where(eight == 2, terms[2], terms[3])))
    term = jnp.where(living, term, 0.0)
    shifted = cell_ref[...] + (CELLS - my_rep * share)
    shifted = jnp.where(shifted >= CELLS, shifted - CELLS, shifted)
    cells = lax.broadcasted_iota(jnp.int32, (CELLS, cap), 0)
    in_cell = jnp.where(cells == shifted, 1.0, 0.0).astype(jnp.bfloat16)
    high, middle_part, low = split3(term)
    total = dot_nt(high, in_cell) + dot_nt(middle_part, in_cell) + dot_nt(low, in_cell)
    for j in range(reps):
        sent_cells[j] = total[0:4, j * share:(j + 1) * share]
    start(cell_copies)

    total = sent_cells[0]
    for k in range(1, reps):
        cell_copies[k - 1].wait()
        total = total + got_cells[k]
    samples_ref[...] = total / (part * reps)
    for k in range(3):
        for j, at in ((0, 0), (1, MOVE + cap)):
            target = pl.ds(at, MOVE)
            for base, sent, got in ((0, sent_place, got_place), (6, sent_speed, got_speed)):
                copy(sent.at[j, k], got.at[j, k], base + 3 * j + k, {"space": near_slab}).wait_recv()
            moved_ref[k, target, :] = got_place[j, k] + TIME_STEP * got_speed[j, k]
            moved_ref[3 + k, target, :] = got_speed[j, k]
    for each in place_far + place_near + speed_far + speed_near:
        each.wait_send()


def assemble_kernel(held_ref, cells_ref, moved_ref, samples_ref, sems):
    copies = [
        pltpu.make_async_copy(held_ref, moved_ref, sems.at[0]),
        pltpu.make_async_copy(cells_ref, samples_ref, sems.at[1]),
    ]
    for each in copies:
        each.start()
    for each in copies:
        each.wait()


def per_device(particles, pair_order, accepted, direction, destination, live_count, cell_index):
    six, _, cap, part = particles.shape
    three = six // 2
    pairs = accepted.shape[2]
    chunk = MOVE
    slabs = lax.axis_size("space")
    reps = lax.axis_size("rep")
    share = CELLS // reps
    f32 = jnp.float32
    out_cap = cap + 2 * MOVE
    in_vmem = pl.BlockSpec(memory_space=pltpu.VMEM)
    in_hbm = pl.BlockSpec(memory_space=pltpu.HBM)
    movers = pltpu.VMEM((2, three, MOVE, part), f32)
    outs = [
        jax.ShapeDtypeStruct((six, out_cap, part), f32),
        jax.ShapeDtypeStruct((4, share), f32),
    ]
    call = pl.pallas_call(
        functools.partial(main_kernel, slabs),
        in_specs=[in_hbm] * 5 + [pl.BlockSpec(memory_space=pltpu.SMEM), in_hbm],
        out_specs=[in_vmem] * 2,
        out_shape=outs,
        scratch_shapes=[
            pltpu.VMEM((six, cap, part), f32),
            pltpu.VMEM((cap, part), jnp.int32),
            pltpu.VMEM((pairs, cap), jnp.int32),
            pltpu.VMEM((pairs, cap), jnp.int32),
            pltpu.VMEM((1, cap), jnp.int32),
            pltpu.VMEM((1, cap), jnp.int32),
            pltpu.VMEM((4, 8, part), f32),
            pltpu.VMEM((chunk, part), jnp.int32),
            pltpu.VMEM((chunk, part), f32),
            pltpu.VMEM((chunk, part), jnp.int32),
            pltpu.VMEM((3, cap, three * part), jnp.bfloat16),
            pltpu.VMEM((cap, part), f32),
            pltpu.VMEM((2 * MOVE, cap), jnp.bfloat16),
            movers,
            movers,
            movers,
            movers,
            pltpu.VMEM((reps, 4, share), f32),
            pltpu.VMEM((reps, 4, share), f32),
            pltpu.SemaphoreType.DMA((9,)),
            pltpu.SemaphoreType.DMA((11 + reps,)),
            pltpu.SemaphoreType.DMA((11 + reps,)),
            pltpu.SemaphoreType.REGULAR,
        ],
        compiler_params=pltpu.CompilerParams(collective_id=0, has_side_effects=True, vmem_limit_bytes=16 * 2 ** 20),
        name="step",
    )
    operands = (
        particles.reshape(six, cap, part),
        pair_order.reshape(cap, part),
        jnp.transpose(accepted.reshape(cap, pairs)),
        jnp.transpose(direction.reshape(cap, pairs)),
        destination.reshape(1, cap),
        live_count,
        cell_index.reshape(1, cap),
    )
    hold = functools.partial(pltpu.with_memory_space_constraint, memory_space=pltpu.HBM)
    operands = [x if x is live_count else hold(x) for x in operands]
    moved, samples = pl.pallas_call(
        assemble_kernel,
        in_specs=[in_vmem] * 2,
        out_specs=[in_hbm] * 2,
        out_shape=outs,
        scratch_shapes=[pltpu.SemaphoreType.DMA((2,))],
        compiler_params=pltpu.CompilerParams(vmem_limit_bytes=2 * 2 ** 20),
        name="assemble",
    )(*call(*operands))
    return (moved[:, None], samples[:, None, :])


def solution(mesh):
    return jax.shard_map(
        per_device,
        mesh=mesh,
        in_specs=(
            P(None, "rep", "space", None),
            P("rep", "space", None),
            P("rep", "space", None),
            P("rep", "space", None),
            P("rep", "space"),
            P("rep", "space"),
            P("rep", "space"),
        ),
        out_specs=(P(None, "rep", "space", None), P(None, "space", "rep")),
        check_vma=False,
    )
```

```python
import functools

import jax
import jax.numpy as jnp
from jax import lax
from jax.experimental import pallas as pl
from jax.experimental.pallas import tpu as pltpu
from jax.sharding import PartitionSpec as P

NDIR = 256
MOVE = 128
CELLS = 256
TIME_STEP = 0.25
GOLDEN_TURN = 2.399963229728653
FAR_STEP = 2
PLACE_GROUPS = ((0, 1), (1, 2))
FAR_GROUPS = ((0, 3),)
NEAR_GROUPS = ((0, 3),)


def take_lanes(values, index):
    return jnp.take_along_axis(values, index, axis=1, mode="promise_in_bounds")


def split3(value):
    high = value.astype(jnp.bfloat16)
    rest = value - high.astype(jnp.float32)
    middle = rest.astype(jnp.bfloat16)
    low = (rest - middle.astype(jnp.float32)).astype(jnp.bfloat16)
    return high, middle, low


def split2(value):
    high = value.astype(jnp.bfloat16)
    return high, (value - high.astype(jnp.float32)).astype(jnp.bfloat16)


def dot(left, right):
    return jnp.dot(left, right, preferred_element_type=jnp.float32)


def dot_nt(left, right):
    return lax.dot_general(left, right, (((1,), (1,)), ((), ())), preferred_element_type=jnp.float32)


def inverse_order(order):
    chunk, part = order.shape
    count = part // 8
    lane = lax.broadcasted_iota(jnp.int32, (chunk, part), 1)
    keys = jnp.transpose((order * part + lane).astype(jnp.float32))
    rows = [keys[8 * i:8 * i + 8] for i in range(count)]
    sublane = lax.broadcasted_iota(jnp.int32, (8, chunk), 0)
    sign = None
    size = 2
    while size <= part:
        wanted = None
        if count <= size < part:
            wanted = jnp.where((sublane & (size // count)) == 0, 1.0, -1.0)
        if sign is not None or wanted is not None:
            flip = wanted if sign is None else sign if wanted is None else sign * wanted
            rows = [row * flip for row in rows]
        sign = wanted
        stride = size // 2
        while stride >= 1:
            if stride >= count:
                apart = stride // count
                is_low = (sublane & apart) == 0
                swapped = [jnp.take_along_axis(row, sublane ^ apart, axis=0, mode="promise_in_bounds") for row in rows]
                rows = [jnp.where(is_low, jnp.minimum(r, o), jnp.maximum(r, o)) for r, o in zip(rows, swapped)]
            else:
                after = list(rows)
                for i in range(count):
                    j = i ^ stride
                    rising = size >= count or (i & size) == 0
                    pick = jnp.minimum if (i < j) == rising else jnp.maximum
                    after[i] = pick(rows[i], rows[j])
                rows = after
            stride //= 2
        size *= 2
    ranked = [(row - ((sublane * count + i) * part).astype(jnp.float32)) for i, row in enumerate(rows)]
    placed = jnp.transpose(jnp.concatenate(ranked, axis=0)).astype(jnp.int32)
    return take_lanes(placed, (lane & (count - 1)) * 8 + lane // count)


def pick_rows(chosen, pieces):
    part = pieces[0].shape[1]
    both = dot(chosen, jnp.concatenate(pieces, axis=1))
    return both[:, :part] + both[:, part:]


def choose_movers(dest_ref, live, goals, chosen_ref):
    cap = dest_ref.shape[1]
    chunk = MOVE
    count = cap // chunk
    lane = lax.broadcasted_iota(jnp.int32, (1, chunk), 1)
    flags = []
    for goal in goals:
        for i in range(count):
            here = dest_ref[:, i * chunk:(i + 1) * chunk]
            flags.append(jnp.where((here == goal) & (lane + i * chunk < live), 1.0, 0.0))
    flags = jnp.concatenate(flags, axis=0)
    row = lax.broadcasted_iota(jnp.int32, (chunk, 2 * chunk), 0)
    column = lax.broadcasted_iota(jnp.int32, (chunk, 2 * chunk), 1)
    sums = jnp.where((row <= column), 1.0, 0.0).astype(jnp.bfloat16)
    counted = dot(flags.astype(jnp.bfloat16), sums)
    slot = lax.broadcasted_iota(jnp.int32, (chunk, chunk), 0)
    for j in range(2):
        before = jnp.zeros((1, chunk), jnp.float32)
        for i in range(count):
            at = j * count + i
            rank = counted[at:at + 1, :chunk] + before
            place = jnp.where(flags[at:at + 1] > 0.0, rank - 1.0, -1.0).astype(jnp.int32)
            chosen_ref[pl.ds(j * MOVE, MOVE), pl.ds(i * chunk, chunk)] = jnp.where(slot == place, 1.0, 0.0).astype(jnp.bfloat16)
            before = before + counted[at:at + 1, chunk:]


def main_kernel(slabs, part_hbm, order_hbm, flag_hbm, turn_hbm, dest_hbm, live_ref, cell_hbm,
                moved_ref, samples_ref, part_ref, order_ref, flag_ref, turn_ref, dest_ref, cell_ref,
                table, packed_t, keep_t, inverse_t, parts, square, chosen_ref,
                sent_place, sent_speed, got_place, got_speed, sent_cells, got_cells,
                load_sem, send_sem, recv_sem, far_sem):
    cap, part = order_ref.shape
    chunk = MOVE
    steps = cap // chunk
    pairs = part // 2
    reps, _, share = sent_cells.shape
    my_slab = lax.axis_index("space")
    my_rep = lax.axis_index("rep")
    odd = lax.rem(my_slab, 2)
    near = odd
    far = 1 - odd
    near_slab = my_slab + 1 - 2 * odd
    far_slab = lax.rem(my_slab + slabs - 1 + 2 * odd, slabs)
    goals = (lax.rem(my_slab + 1, slabs), lax.rem(my_slab + slabs - 1, slabs))
    is_end = (my_slab == 0) | (my_slab == slabs - 1)
    assert slabs % 4 == 0
    quarter = lax.rem(my_slab, 4)
    is_hub = quarter == 2
    is_last = my_slab == 0
    is_first = my_slab == 1
    live = live_ref[0, 0]

    loads = []

    def load(source, target):
        each = pltpu.make_async_copy(source, target, load_sem.at[len(loads)])
        each.start()
        loads.append(each)
        return each

    dest_load = load(dest_hbm, dest_ref)
    place_loads = [load(part_hbm.at[k], part_ref.at[k]) for k in range(3)]
    turn_load = load(turn_hbm, turn_ref)
    flag_load = load(flag_hbm, flag_ref)
    order_load = load(order_hbm, order_ref)
    speed_load = load(part_hbm.at[pl.ds(3, 3)], part_ref.at[pl.ds(3, 3)])
    cell_load = load(cell_hbm, cell_ref)

    def copy(source, target, k, device):
        return pltpu.make_async_remote_copy(
            src_ref=source, dst_ref=target, send_sem=send_sem.at[k], recv_sem=recv_sem.at[k],
            device_id=device, device_id_type=pl.DeviceIdType.MESH,
        )

    def mover_copies(sent, got, base, j, device, groups):
        return [
            copy(sent.at[j, pl.ds(k, n)], got.at[j, pl.ds(k, n)], base + 3 * j + k, {"space": device}) for k, n in groups
        ]

    place_far = mover_copies(sent_place, got_place, 0, far, far_slab, PLACE_GROUPS)
    place_near = mover_copies(sent_place, got_place, 0, near, near_slab, PLACE_GROUPS)
    speed_far = mover_copies(sent_speed, got_speed, 6, far, far_slab, FAR_GROUPS)
    speed_near = mover_copies(sent_speed, got_speed, 6, near, near_slab, NEAR_GROUPS)
    cell_copies = [
        copy(sent_cells.at[k], got_cells.at[k], 11 + k, {"rep": lax.rem(my_rep + k, reps)}) for k in range(1, reps)
    ]

    def start(copies):
        for each in copies:
            each.start()

    barrier = pltpu.get_barrier_semaphore()

    def greet(**device):
        pl.semaphore_signal(barrier, inc=1, device_id=device, device_id_type=pl.DeviceIdType.MESH)

    greet(space=near_slab)
    for k in range(1, reps):
        greet(rep=lax.rem(my_rep + k, reps))

    @pl.when(quarter == 0)
    def _():
        greet(space=lax.rem(my_slab + slabs - 2, slabs))

    @pl.when(quarter == 1)
    def _():
        greet(space=far_slab)

    dest_load.wait()
    choose_movers(dest_ref, live, goals, chosen_ref)
    for k in range(3):
        place_loads[k].wait()
        sent = pick_rows(chosen_ref[...], split2(part_ref[k]))
        sent_place[0, k] = sent[:MOVE]
        sent_place[1, k] = sent[MOVE:]
        if k == 0:
            @pl.when(is_hub)
            def _():
                pl.semaphore_wait(barrier, 2 + reps)
                for other in (near_slab, far_slab, lax.rem(my_slab + 2, slabs)):
                    pl.semaphore_signal(far_sem, inc=1, device_id={"space": other}, device_id_type=pl.DeviceIdType.MESH)

            @pl.when(jnp.logical_not(is_hub))
            def _():
                pl.semaphore_wait(barrier, reps)

        for i, (first, count) in enumerate(PLACE_GROUPS):
            if first + count == k + 1:
                place_near[i].start()

                @pl.when(is_hub)
                def _(i=i):
                    place_far[i].start()

    for half in range(2):
        turns = (lax.broadcasted_iota(jnp.int32, (8, part), 1) + half * part).astype(jnp.float32)
        height = 1.0 - (2.0 * turns + 1.0) / NDIR
        radius = jnp.sqrt(1.0 - height * height)
        angle = turns * GOLDEN_TURN
        table[half] = radius * jnp.cos(angle)
        table[half + 2] = radius * jnp.sin(angle)

    turn_load.wait()
    flag_load.wait()
    order_load.wait()
    speed_load.wait()

    def chunk_step(step, carry):
        at = pl.multiple_of(step * chunk, chunk)
        here = pl.ds(at, chunk)
        pair_code = turn_ref[:, here] + NDIR * flag_ref[:, here]
        packed_t[...] = jnp.transpose(jnp.concatenate([pair_code, pair_code], axis=0))
        slots = lax.broadcasted_iota(jnp.int32, (1, chunk), 1) + at
        staying = (dest_ref[:, here] == my_slab) & (slots < live)
        stay_rows = jnp.broadcast_to(jnp.where(staying, 1.0, 0.0), (part, chunk))
        keep_t[...] = jnp.transpose(stay_rows)
        inverse_t[...] = inverse_order(order_ref[here, :])

        order = order_ref[here, :]
        inverse = inverse_t[...]
        partner = take_lanes(order, inverse ^ pairs)
        code = take_lanes(packed_t[...], inverse & (pairs - 1))
        taken = code >= NDIR
        turn = code & (NDIR - 1)
        low_index = turn & (part - 1)
        is_high = turn >= part
        wide = (chunk, part)
        tables = [jnp.broadcast_to(table[k, 0:1, :], wide) for k in range(4)]
        unit_x = jnp.where(is_high, take_lanes(tables[1], low_index), take_lanes(tables[0], low_index))
        unit_y = jnp.where(is_high, take_lanes(tables[3], low_index), take_lanes(tables[2], low_index))
        unit_z = 1.0 - (2.0 * turn.astype(jnp.float32) + 1.0) / NDIR
        old = [part_ref[3 + k, here, :] for k in range(3)]
        other = [take_lanes(v, partner) for v in old]
        relative = [a - b for a, b in zip(old, other)]
        speed = jnp.sqrt(relative[0] * relative[0] + relative[1] * relative[1] + relative[2] * relative[2])
        half_speed = jnp.where(inverse < pairs, 0.5, -0.5) * speed
        new = [
            jnp.where(taken, 0.5 * (a + b) + half_speed * u, a)
            for a, b, u in zip(old, other, (unit_x, unit_y, unit_z))
        ]
        keep = keep_t[...] > 0.0
        target = pl.ds(pl.multiple_of(MOVE + at, chunk), chunk)
        square[here, :] = new[0] * new[0] + new[1] * new[1] + new[2] * new[2]
        for k in range(3):
            moved_ref[k, target, :] = jnp.where(keep, part_ref[k, here, :] + TIME_STEP * new[k], 0.0)
            moved_ref[3 + k, target, :] = jnp.where(keep, new[k], 0.0)
            for j, piece in enumerate(split3(new[k])):
                parts[j, here, pl.ds(k * part, part)] = piece

        @pl.when((step == jnp.where(is_last, steps - 1, FAR_STEP)) & jnp.logical_not(is_hub))
        def _():
            pl.semaphore_wait(far_sem, 1)
            start(place_far)

        return carry

    lax.fori_loop(0, steps, chunk_step, 0)

    for k in range(3):
        sent = pick_rows(chosen_ref[...], [parts[j, :, pl.ds(k * part, part)] for j in range(2)])
        sent_speed[0, k] = sent[:MOVE]
        sent_speed[1, k] = sent[MOVE:]

    @pl.when(jnp.logical_not(is_first))
    def _():
        start(speed_far)

    start(speed_near)

    @pl.when(is_first)
    def _():
        start(speed_far)

    cell_load.wait()
    living = lax.broadcasted_iota(jnp.int32, (1, cap), 1) < live
    ones = jnp.ones((8, part), jnp.bfloat16)
    eight = lax.broadcasted_iota(jnp.int32, (8, cap), 0)
    terms = []
    for k in range(3):
        here = pl.ds(k * part, part)
        terms.append(dot_nt(ones, parts[0, :, here]) + dot_nt(ones, parts[1, :, here]) + dot_nt(ones, parts[2, :, here]))
    pieces = split3(square[...])
    terms.append(dot_nt(ones, pieces[0]) + dot_nt(ones, pieces[1]) + dot_nt(ones, pieces[2]))
    term = jnp.where(eight == 0, terms[0], jnp.where(eight == 1, terms[1], jnp.where(eight == 2, terms[2], terms[3])))
    term = jnp.where(living, term, 0.0)
    shifted = cell_ref[...] + (CELLS - my_rep * share)
    shifted = jnp.where(shifted >= CELLS, shifted - CELLS, shifted)
    cells = lax.broadcasted_iota(jnp.int32, (CELLS, cap), 0)
    in_cell = jnp.where(cells == shifted, 1.0, 0.0).astype(jnp.bfloat16)
    high, middle_part, low = split3(term)
    total = dot_nt(high, in_cell) + dot_nt(middle_part, in_cell) + dot_nt(low, in_cell)
    for j in range(reps):
        sent_cells[j] = total[0:4, j * share:(j + 1) * share]
    start(cell_copies)

    total = sent_cells[0]
    for k in range(1, reps):
        cell_copies[k - 1].wait()
        total = total + got_cells[k]
    samples_ref[...] = total / (part * reps)
    for k, n in PLACE_GROUPS:
        for j in range(2):
            here = pl.ds(k, n)
            copy(sent_place.at[j, here], got_place.at[j, here], 3 * j + k, {"space": near_slab}).wait_recv()

    def take(base, groups, j):
        for k, n in groups:
            here = pl.ds(k, n)
            copy(sent_speed.at[j, here], got_speed.at[j, here], 6 + 3 * j + k, {"space": near_slab}).wait_recv()
            for i in range(k, k + n):
                moved_ref[i, pl.ds(base, MOVE), :] = got_place[j, i] + TIME_STEP * got_speed[j, i]
                moved_ref[3 + i, pl.ds(base, MOVE), :] = got_speed[j, i]

    @pl.when(odd == 0)
    def _():
        take(0, FAR_GROUPS, 0)
        take(MOVE + cap, NEAR_GROUPS, 1)

    @pl.when(odd == 1)
    def _():
        take(MOVE + cap, FAR_GROUPS, 1)
        take(0, NEAR_GROUPS, 0)

    for each in place_far + place_near + speed_far + speed_near:
        each.wait_send()


def assemble_kernel(held_ref, cells_ref, moved_ref, samples_ref, sems):
    copies = [
        pltpu.make_async_copy(held_ref, moved_ref, sems.at[0]),
        pltpu.make_async_copy(cells_ref, samples_ref, sems.at[1]),
    ]
    for each in copies:
        each.start()
    for each in copies:
        each.wait()


def per_device(particles, pair_order, accepted, direction, destination, live_count, cell_index):
    six, _, cap, part = particles.shape
    three = six // 2
    pairs = accepted.shape[2]
    chunk = MOVE
    slabs = lax.axis_size("space")
    reps = lax.axis_size("rep")
    share = CELLS // reps
    f32 = jnp.float32
    out_cap = cap + 2 * MOVE
    in_vmem = pl.BlockSpec(memory_space=pltpu.VMEM)
    in_hbm = pl.BlockSpec(memory_space=pltpu.HBM)
    movers = pltpu.VMEM((2, three, MOVE, part), f32)
    outs = [
        jax.ShapeDtypeStruct((six, out_cap, part), f32),
        jax.ShapeDtypeStruct((4, share), f32),
    ]
    call = pl.pallas_call(
        functools.partial(main_kernel, slabs),
        in_specs=[in_hbm] * 5 + [pl.BlockSpec(memory_space=pltpu.SMEM), in_hbm],
        out_specs=[in_vmem] * 2,
        out_shape=outs,
        scratch_shapes=[
            pltpu.VMEM((six, cap, part), f32),
            pltpu.VMEM((cap, part), jnp.int32),
            pltpu.VMEM((pairs, cap), jnp.int32),
            pltpu.VMEM((pairs, cap), jnp.int32),
            pltpu.VMEM((1, cap), jnp.int32),
            pltpu.VMEM((1, cap), jnp.int32),
            pltpu.VMEM((4, 8, part), f32),
            pltpu.VMEM((chunk, part), jnp.int32),
            pltpu.VMEM((chunk, part), f32),
            pltpu.VMEM((chunk, part), jnp.int32),
            pltpu.VMEM((3, cap, three * part), jnp.bfloat16),
            pltpu.VMEM((cap, part), f32),
            pltpu.VMEM((2 * MOVE, cap), jnp.bfloat16),
            movers,
            movers,
            movers,
            movers,
            pltpu.VMEM((reps, 4, share), f32),
            pltpu.VMEM((reps, 4, share), f32),
            pltpu.SemaphoreType.DMA((9,)),
            pltpu.SemaphoreType.DMA((11 + reps,)),
            pltpu.SemaphoreType.DMA((11 + reps,)),
            pltpu.SemaphoreType.REGULAR,
        ],
        compiler_params=pltpu.CompilerParams(collective_id=0, has_side_effects=True, vmem_limit_bytes=16 * 2 ** 20),
        name="step",
    )
    operands = (
        particles.reshape(six, cap, part),
        pair_order.reshape(cap, part),
        jnp.transpose(accepted.reshape(cap, pairs)),
        jnp.transpose(direction.reshape(cap, pairs)),
        destination.reshape(1, cap),
        live_count,
        cell_index.reshape(1, cap),
    )
    hold = functools.partial(pltpu.with_memory_space_constraint, memory_space=pltpu.HBM)
    operands = [x if x is live_count else hold(x) for x in operands]
    moved, samples = pl.pallas_call(
        assemble_kernel,
        in_specs=[in_vmem] * 2,
        out_specs=[in_hbm] * 2,
        out_shape=outs,
        scratch_shapes=[pltpu.SemaphoreType.DMA((2,))],
        compiler_params=pltpu.CompilerParams(vmem_limit_bytes=2 * 2 ** 20),
        name="assemble",
    )(*call(*operands))
    return (moved[:, None], samples[:, None, :])


def solution(mesh):
    return jax.shard_map(
        per_device,
        mesh=mesh,
        in_specs=(
            P(None, "rep", "space", None),
            P("rep", "space", None),
            P("rep", "space", None),
            P("rep", "space", None),
            P("rep", "space"),
            P("rep", "space"),
            P("rep", "space"),
        ),
        out_specs=(P(None, "rep", "space", None), P(None, "space", "rep")),
        check_vma=False,
    )
```
